32 devices in a mesh: dp: 8 (over z, x), mp: 4 (over y, core).
Axes of the slice: x: 2, y: 2, z: 4, core: 2. Of those that a mesh axis runs over, the one named last changes fastest.
Arguments:
- media: bfloat16 [16, 8, 256, 1024], P('dp'), may hold values from -6 to 6
- latents: bfloat16 [64, 1024], replicated, may hold values from -6 to 6
- time_embed: bfloat16 [8, 1024], replicated, may hold values from -5 to 5
- media_gain: float32 [2, 1024], replicated, may hold values from 0.25 to 1.75
- latent_gain: float32 [2, 1024], replicated, may hold values from 0.25 to 1.75
- ffn_gain: float32 [2, 1024], replicated, may hold values from 0.25 to 1.75
- out_gain: float32 [1024], replicated, may hold values from 0.25 to 1.75
- w_query: bfloat16 [2, 1024, 512], P(None, 'dp', 'mp'), may hold values from -0.1875 to 0.1875
- w_key: bfloat16 [2, 1024, 512], P(None, 'dp', 'mp'), may hold values from -0.1875 to 0.1875
- w_value: bfloat16 [2, 1024, 512], P(None, 'dp', 'mp'), may hold values from -0.1875 to 0.1875
- w_out: bfloat16 [2, 512, 1024], P(None, 'mp', 'dp'), may hold values from -0.25 to 0.25
- w_up: bfloat16 [2, 1024, 4096], P(None, 'dp', 'mp'), may hold values from -0.1875 to 0.1875
- w_down: bfloat16 [2, 4096, 1024], P(None, 'mp', 'dp'), may hold values from -0.09375 to 0.09375
Outputs:
- resampled: bfloat16 [16, 64, 1024], P('dp')
The draws below stay inside these ranges and needn't reach their ends.
All inputs are finite; a program needn't handle non-finite values.
Results may differ from the reference program's by a relative error of at most 0.013.
Values may be sent and summed in bfloat16 or wider, within the bound.
A program may use at most 128 MiB of HBM per device.

```python
import jax
import jax.numpy as jnp
from jax import lax

D = 1024
HEADS = 8
HEAD = 64
FF = 4096
NLAT = 64
FRAMES = 8
PATCHES = 256
LAYERS = 2
INNER = 512
SAMPLES = 16


def levels(stream_key, extent, cuts, low, largest):
    level, own = 1.0, jax.random.fold_in(stream_key, 6)
    for dim, shards_of in cuts:
        steps = jnp.exp(jax.random.uniform(jax.random.fold_in(own, dim), (shards_of,), jnp.float32, low / len(cuts), largest / len(cuts)))
        level = level * jnp.repeat(steps, extent[dim] // shards_of).reshape([-1 if axis == dim else 1 for axis in range(len(extent))])
    return level


def bell_draw(own_key, dims, scale, limit, cuts=(), dtype=jnp.bfloat16):
    entries = scale * jax.random.normal(own_key, dims, jnp.float32)
    if cuts:
        entries = entries * levels(own_key, dims, cuts, -0.22, 0.18)
    return jnp.clip(entries, -limit, limit).astype(dtype)


def setup_inputs(seed: int = 0) -> dict:
    key_of = jax.random.split(jax.random.key(seed), 14)
    return {
        "media": bell_draw(key_of[0], (SAMPLES, FRAMES, PATCHES, D), 1.0, 6.0, ((0, 8),)),
        "latents": bell_draw(key_of[1], (NLAT, D), 1.0, 6.0),
        "time_embed": bell_draw(key_of[2], (FRAMES, D), 0.7, 5.0),
        "media_gain": jnp.clip(1.0 + 0.15 * jax.random.normal(key_of[3], (LAYERS, D), jnp.float32), 0.25, 1.75),
        "latent_gain": jnp.clip(1.0 + 0.15 * jax.random.normal(key_of[4], (LAYERS, D), jnp.float32), 0.25, 1.75),
        "ffn_gain": jnp.clip(1.0 + 0.15 * jax.random.normal(key_of[5], (LAYERS, D), jnp.float32), 0.25, 1.75),
        "out_gain": jnp.clip(1.0 + 0.15 * jax.random.normal(key_of[6], (D,), jnp.float32), 0.25, 1.75),
        "w_query": bell_draw(key_of[7], (LAYERS, D, INNER), D ** -0.5, 0.1875, ((1, 8), (2, 4))),
        "w_key": bell_draw(key_of[8], (LAYERS, D, INNER), D ** -0.5, 0.1875, ((1, 8), (2, 4))),
        "w_value": bell_draw(key_of[9], (LAYERS, D, INNER), D ** -0.5, 0.1875, ((1, 8), (2, 4))),
        "w_out": bell_draw(key_of[10], (LAYERS, INNER, D), INNER ** -0.5, 0.25, ((1, 4), (2, 8))),
        "w_up": bell_draw(key_of[11], (LAYERS, D, FF), D ** -0.5, 0.1875, ((1, 8), (2, 4))),
        "w_down": bell_draw(key_of[12], (LAYERS, FF, D), FF ** -0.5, 0.09375, ((1, 4), (2, 8))),
    }


def layer_norm(values, gain):
    center = values - lax.optimization_barrier(jnp.mean(values, axis=-1, keepdims=True))
    spread = lax.optimization_barrier(jnp.mean(center * center, axis=-1, keepdims=True))
    return center * lax.rsqrt(spread + 1e-05) * gain

def reference(media, latents, time_embed, media_gain, latent_gain, ffn_gain, out_gain, w_query, w_key, w_value, w_out, w_up, w_down):
    scale = HEAD ** (-0.5)

    def one_sample(sample):
        flat = (sample.astype(jnp.float32) + time_embed.astype(jnp.float32)[:, None, :]).reshape(FRAMES * PATCHES, D)
        state = latents.astype(jnp.float32)
        for layer in range(LAYERS):
            media_normed = layer_norm(flat, media_gain[layer]).astype(jnp.bfloat16)
            latent_normed = layer_norm(state, latent_gain[layer]).astype(jnp.bfloat16)
            queries = (jnp.dot(latent_normed, w_query[layer], preferred_element_type=jnp.float32) * scale).astype(jnp.bfloat16)
            inputs = jnp.concatenate([media_normed, latent_normed], axis=0)
            keys = jnp.dot(inputs, w_key[layer], preferred_element_type=jnp.float32).astype(jnp.bfloat16)
            values = jnp.dot(inputs, w_value[layer], preferred_element_type=jnp.float32).astype(jnp.bfloat16)
            qheads = queries.astype(jnp.float32).reshape(NLAT, HEADS, HEAD)
            kheads = keys.astype(jnp.float32).reshape(-1, HEADS, HEAD)
            vheads = values.astype(jnp.float32).reshape(-1, HEADS, HEAD)
            scores = jnp.einsum('qhd,khd->hqk', qheads, kheads)
            probs = jax.nn.softmax(scores, axis=-1).astype(jnp.bfloat16)
            attended = jnp.einsum('hqk,khd->qhd', probs.astype(jnp.float32), vheads).astype(jnp.bfloat16).reshape(NLAT, HEADS * HEAD)
            state = state + jnp.dot(attended, w_out[layer], preferred_element_type=jnp.float32)
            ffn_normed = layer_norm(state, ffn_gain[layer]).astype(jnp.bfloat16)
            hidden = jax.nn.gelu(jnp.dot(ffn_normed, w_up[layer], preferred_element_type=jnp.float32), approximate=False).astype(jnp.bfloat16)
            state = state + jnp.dot(hidden, w_down[layer], preferred_element_type=jnp.float32)
        return layer_norm(state, out_gain).astype(jnp.bfloat16)
    return lax.map(one_sample, media)
```

```python
import functools

import jax
import jax.numpy as jnp
from jax import lax
from jax.experimental import pallas as pl
from jax.experimental.pallas import tpu as pltpu
from jax.sharding import PartitionSpec as P

MESH = pl.DeviceIdType.MESH

HEAD = 64
LAYERS = 2


def layer_norm(values, gain):
    center = values - jnp.mean(values, axis=-1, keepdims=True)
    spread = jnp.mean(center * center, axis=-1, keepdims=True)
    return center * lax.rsqrt(spread + 1e-05) * gain


def matmul(left, right):
    return jnp.dot(left, right, preferred_element_type=jnp.float32)


def on_device(
    media,
    latents,
    time_embed,
    media_gain,
    latent_gain,
    ffn_gain,
    out_gain,
    w_query,
    w_key,
    w_value,
    w_out,
    w_up,
    w_down,
):
    samples = media.shape[0]
    frames = media.shape[1]
    patches = media.shape[2]
    width = media.shape[3]
    count = latents.shape[0]
    head_size = HEAD
    local_heads = w_query.shape[2] // head_size
    scale = head_size ** (-0.5)
    tokens = frames * patches
    flat = (media.astype(jnp.float32) + time_embed.astype(jnp.float32)[None, :, None, :]).reshape(
        samples * tokens, width
    )
    state = jnp.broadcast_to(latents.astype(jnp.float32)[None], (samples, count, width)).reshape(
        samples * count, width
    )
    row_parts = (
        lax.all_gather(w_query, "dp", axis=1, tiled=True),
        lax.all_gather(w_key, "dp", axis=1, tiled=True),
        lax.all_gather(w_value, "dp", axis=1, tiled=True),
        lax.all_gather(w_up, "dp", axis=1, tiled=True),
    )
    col_parts = (
        lax.all_gather(w_out, "dp", axis=2, tiled=True),
        lax.all_gather(w_down, "dp", axis=2, tiled=True),
    )

    def full_rows(values, gain):
        normed = layer_norm(values, gain).astype(jnp.bfloat16)
        return normed

    def add_update(current, partial_value):
        return current + lax.psum(partial_value.astype(jnp.bfloat16), "mp").astype(jnp.float32)

    for layer in range(LAYERS):
        query_weight = row_parts[0][layer]
        key_weight = row_parts[1][layer]
        value_weight = row_parts[2][layer]
        up_weight = row_parts[3][layer]
        out_weight = col_parts[0][layer]
        down_weight = col_parts[1][layer]
        media_normed = layer_norm(flat, media_gain[layer]).astype(jnp.bfloat16)
        latent_normed = full_rows(state, latent_gain[layer])
        query = matmul(latent_normed, query_weight)
        key_media = matmul(media_normed, key_weight)
        value_media = matmul(media_normed, value_weight)
        key_latent = matmul(latent_normed, key_weight)
        value_latent = matmul(latent_normed, value_weight)
        queries = (
            (query * scale).astype(jnp.bfloat16).reshape(samples, count, local_heads, head_size)
        )
        keys = jnp.concatenate(
            [
                key_media.astype(jnp.bfloat16).reshape(samples, tokens, local_heads, head_size),
                key_latent.astype(jnp.bfloat16).reshape(samples, count, local_heads, head_size),
            ],
            axis=1,
        )
        values = jnp.concatenate(
            [
                value_media.astype(jnp.bfloat16).reshape(samples, tokens, local_heads, head_size),
                value_latent.astype(jnp.bfloat16).reshape(samples, count, local_heads, head_size),
            ],
            axis=1,
        )
        scores = jnp.einsum("sqhd,skhd->shqk", queries, keys, preferred_element_type=jnp.float32)
        probs = jax.nn.softmax(scores, axis=-1).astype(jnp.bfloat16)
        attended = jnp.einsum("shqk,skhd->sqhd", probs, values, preferred_element_type=jnp.float32)
        attended = attended.astype(jnp.bfloat16).reshape(samples * count, local_heads * head_size)
        state = add_update(state, matmul(attended, out_weight))
        ffn_normed = full_rows(state, ffn_gain[layer])
        hidden = jax.nn.gelu(matmul(ffn_normed, up_weight), approximate=False).astype(jnp.bfloat16)
        state = add_update(state, matmul(hidden, down_weight))
    final = layer_norm(state, out_gain).astype(jnp.bfloat16)
    return final.reshape(samples, count, width)


def fused_kernel(
    n, groups,
    media, latents, time_embed, media_gain, latent_gain, ffn_gain, out_gain,
    w_query, w_key, w_value, w_out, w_up, w_down,
    out,
    frames_in, normed_next, kv, g_qkv, g_out, g_up, g_down, state,
    part, rs_in, ag_in,
    media_sem, own_sem, send_sem, recv_sem, rs_send, rs_recv, ag_send, ag_recv,
):
    samples, frames, patches, width = media.shape
    count = latents.shape[0]
    tokens = frames * patches
    inner = w_query.shape[2]
    heads = inner // HEAD
    depth = w_query.shape[1]
    hidden = w_up.shape[2]
    half = hidden // 2
    ring = n // 2
    me = lax.axis_index("dp")
    mine = lax.axis_index("mp")
    along, across = me // 2, me % 2

    def index(a, b):
        return lax.rem(a + 2 * ring, ring) * 2 + b

    for target in (index(along, 1 - across), index(along + 1, across), index(along - 1, across)):
        pl.semaphore_signal(pltpu.get_barrier_semaphore(), inc=1, device_id={"dp": target}, device_id_type=MESH)
    for k in range(1, groups):
        pl.semaphore_signal(
            pltpu.get_barrier_semaphore(), inc=1, device_id={"mp": lax.rem(mine + k, groups)}, device_id_type=MESH
        )

    units = []
    for layer in range(LAYERS):
        if layer == 0:
            units += [("qkv", 0, 0), ("qkv", 1, 1)]
        units += [("out", layer, layer), ("up", layer, 0), ("up", layer, 1), ("down", layer, 0), ("down", layer, 1)]
    where = {unit: i for i, unit in enumerate(units)}

    def span(origin, size):
        return pl.ds(pl.multiple_of(origin * size, size), size)

    def piece(u, origin):
        kind, layer, part_of = units[u]
        if kind == "qkv":
            return g_qkv.at[layer, span(origin, depth), :]
        if kind == "out":
            return g_out.at[layer, :, span(origin, depth)]
        if kind == "up":
            return g_up.at[layer, span(origin, depth), pl.ds(part_of * half, half)]
        return g_down.at[layer, pl.ds(part_of * half, half), span(origin, depth)]

    def own_copies(u):
        kind, layer, part_of = units[u]
        if kind == "qkv":
            return [
                pltpu.make_async_copy(
                    w.at[layer], g_qkv.at[layer, span(me, depth), pl.ds(i * inner, inner)], own_sem.at[u, i]
                )
                for i, w in enumerate((w_query, w_key, w_value))
            ]
        if kind == "out":
            source = w_out.at[layer]
        elif kind == "up":
            source = w_up.at[layer, :, pl.ds(part_of * half, half)]
        else:
            source = w_down.at[layer, pl.ds(part_of * half, half), :]
        return [pltpu.make_async_copy(source, piece(u, me), own_sem.at[u, 0])]

    def turn(u):
        return 1 if units[u][2] == 0 else -1

    def sending(u, s, other, to_ring):
        r = turn(u)
        ref = piece(u, index(along - r * s, 1 - across if other else across))
        if to_ring:
            target, slot = index(along + r, across), recv_sem.at[u, s + 1, other]
        else:
            target, slot = index(along, 1 - across), recv_sem.at[u, s, 1 - other]
        return pltpu.make_async_remote_copy(
            src_ref=ref, dst_ref=ref, send_sem=send_sem.at[u, s, other, int(to_ring)], recv_sem=slot,
            device_id={"dp": target}, device_id_type=MESH,
        )

    started = []

    def send(*which):
        copy = sending(*which)
        copy.start()
        started.append(copy)

    def arrived(u, s, other):
        r = turn(u)
        ref = piece(u, index(along - r * s, 1 - across if other else across))
        pltpu.make_async_remote_copy(
            src_ref=ref, dst_ref=ref, send_sem=send_sem.at[u, s, other, 0], recv_sem=recv_sem.at[u, s, other],
            device_id={"dp": index(along, 1 - across)}, device_id_type=MESH,
        ).wait_recv()

    def pair_first(u):
        return units[u][0] == "up" and units[u][2] == 1

    def event(u, s):
        if s == 0:
            for copy in own_copies(u):
                copy.wait()
            send(u, 0, 0, True)
            send(u, 0, 0, False)
            return
        if pair_first(u):
            arrived(u, s - 1, 1)
            send(u, s - 1, 1, True)
            arrived(u, s, 0)
            if s < ring - 1:
                send(u, s, 0, True)
        else:
            arrived(u, s, 0)
            if s < ring - 1:
                send(u, s, 0, True)
            send(u, s, 0, False)

    def complete(u):
        if pair_first(u):
            arrived(u, ring - 1, 1)
        else:
            for s in range(ring):
                arrived(u, s, 1)

    slots = {}
    for u in range(len(units)):
        for s in range(ring):
            slots.setdefault(u + s + (1 if s else 0), []).append((u, s))
    clock = [0]

    def advance(until):
        while clock[0] <= until:
            for u, s in sorted(slots.get(clock[0], []), key=lambda e: (e[1] > 0, e[0])):
                event(u, s)
            clock[0] += 1

    def need(*unit):
        u = where[unit]
        advance(u + ring)
        complete(u)

    for u in range(len(units)):
        for copy in own_copies(u):
            copy.start()

    def frame_copy(i):
        return pltpu.make_async_copy(media.at[i // frames, i % frames], frames_in.at[i], media_sem.at[i])

    @pl.loop(0, samples * frames)
    def _(i):
        frame_copy(i).start()

    pl.semaphore_wait(pltpu.get_barrier_semaphore(), 3 + groups - 1)
    advance(1)

    state[...] = jnp.concatenate([latents[...].astype(jnp.float32)] * samples, axis=0)

    def norm_frames(low, high):
        @pl.loop(low, high)
        def _(i):
            frame_copy(i).wait()

            @pl.loop(0, patches // 64)
            def _(j):
                rows = pl.ds(pl.multiple_of(j * 64, 64), 64)
                flat = frames_in[i, rows, :].astype(jnp.float32) + time_embed[pl.ds(lax.rem(i, frames), 1), :]
                center = flat - jnp.mean(flat, axis=-1, keepdims=True)
                spread = jnp.mean(center * center, axis=-1, keepdims=True)
                scaled = center * lax.rsqrt(spread + 1e-05)
                frames_in[i, rows, :] = (scaled * media_gain[0:1, :]).astype(jnp.bfloat16)
                normed_next[i, rows, :] = (scaled * media_gain[1:2, :]).astype(jnp.bfloat16)

    def project(layer):
        normed = frames_in if layer == 0 else normed_next

        @pl.loop(0, samples * frames)
        def _(i):
            both = matmul(normed[i], g_qkv[layer, :, inner : 3 * inner])
            rows = pl.ds(pl.multiple_of(lax.rem(i, frames) * patches, patches), patches)
            kv[layer, i // frames, rows, :] = both.astype(jnp.bfloat16)

    def attend(layer):
        normed = layer_norm(state[...], latent_gain[layer : layer + 1, :]).astype(jnp.bfloat16)
        own = matmul(normed, g_qkv[layer])
        queries = (own[:, :inner] * (HEAD ** (-0.5))).astype(jnp.bfloat16)
        own_kv = own[:, inner:].astype(jnp.bfloat16)
        lane = lax.broadcasted_iota(jnp.int32, (count, inner), 1) // HEAD
        dims = (((1,), (1,)), ((), ()))
        results = []
        for b in range(samples):
            q = queries[b * count : (b + 1) * count]
            stacked = jnp.concatenate([jnp.where(lane == h, q, jnp.zeros_like(q)) for h in range(heads)], axis=0)
            k_own = own_kv[b * count : (b + 1) * count, :inner]
            v_own = own_kv[b * count : (b + 1) * count, inner:]
            s_far = lax.dot_general(stacked, kv[layer, b, :, :inner], dims, preferred_element_type=jnp.float32)
            s_own = lax.dot_general(stacked, k_own, dims, preferred_element_type=jnp.float32)
            top = jnp.maximum(jnp.max(s_far, axis=-1, keepdims=True), jnp.max(s_own, axis=-1, keepdims=True))
            e_far, e_own = jnp.exp(s_far - top), jnp.exp(s_own - top)
            total = jnp.sum(e_far, axis=-1, keepdims=True) + jnp.sum(e_own, axis=-1, keepdims=True)
            inverse = 1.0 / total
            mixed = matmul((e_far * inverse).astype(jnp.bfloat16), kv[layer, b, :, inner:])
            mixed += matmul((e_own * inverse).astype(jnp.bfloat16), v_own)
            result = mixed[:count]
            for h in range(1, heads):
                result = jnp.where(lane == h, mixed[h * count : (h + 1) * count], result)
            results.append(result.astype(jnp.bfloat16))
        return jnp.concatenate(results, axis=0)

    rows_each = samples * count // groups

    def add_update(a, update):
        part[a] = update.astype(jnp.bfloat16).reshape(groups, rows_each, width)
        first = []
        for k in range(1, groups):
            peer = lax.rem(mine + k, groups)
            copy = pltpu.make_async_remote_copy(
                src_ref=part.at[a, peer], dst_ref=rs_in.at[a, k - 1],
                send_sem=rs_send.at[a, k - 1], recv_sem=rs_recv.at[a, k - 1],
                device_id={"mp": peer}, device_id_type=MESH,
            )
            copy.start()
            started.append(copy)
            first.append(copy)
        total = part[a, mine].astype(jnp.float32)
        for k, copy in enumerate(first):
            copy.wait_recv()
            total += rs_in[a, k].astype(jnp.float32)
        ag_in[a, mine] = total.astype(jnp.bfloat16)
        second = []
        for k in range(1, groups):
            copy = pltpu.make_async_remote_copy(
                src_ref=ag_in.at[a, mine], dst_ref=ag_in.at[a, mine],
                send_sem=ag_send.at[a, k - 1], recv_sem=ag_recv.at[a, k - 1],
                device_id={"mp": lax.rem(mine + k, groups)}, device_id_type=MESH,
            )
            copy.start()
            started.append(copy)
            second.append(copy)
        for copy in second:
            copy.wait_recv()
        state[...] += ag_in[a].astype(jnp.float32).reshape(samples * count, width)

    middle = samples * frames // 2
    norm_frames(0, middle)
    advance(2)
    norm_frames(middle, samples * frames)
    for layer in range(LAYERS):
        if layer == 0:
            need("qkv", 0, 0)
            project(0)
        attended = attend(layer)
        if layer == 0:
            need("qkv", 1, 1)
            project(1)
        need("out", layer, layer)
        add_update(2 * layer, matmul(attended, g_out[layer]))
        normed = layer_norm(state[...], ffn_gain[layer : layer + 1, :]).astype(jnp.bfloat16)
        active = []
        for h in range(2):
            need("up", layer, h)
            value = matmul(normed, g_up[layer, :, h * half : (h + 1) * half])
            active.append((0.5 * value * (1.0 + lax.erf(value * (0.5**0.5)))).astype(jnp.bfloat16))
        update = None
        for h in range(2):
            need("down", layer, h)
            term = matmul(active[h], g_down[layer, h * half : (h + 1) * half, :])
            update = term if update is None else update + term
        add_update(2 * layer + 1, update)
    final = layer_norm(state[...], out_gain[...]).astype(jnp.bfloat16)
    out[...] = final.reshape(samples, count, width)
    for copy in started:
        copy.wait_send()


def fused(n, groups, media, latents, time_embed, media_gain, latent_gain, ffn_gain, out_gain,
          w_query, w_key, w_value, w_out, w_up, w_down):
    samples, frames, patches, width = media.shape
    count = latents.shape[0]
    inner = w_query.shape[2]
    hidden = w_up.shape[2]
    ring = n // 2
    rows_each = samples * count // groups
    units = LAYERS * 6
    bf16 = jnp.bfloat16
    dma = pltpu.SemaphoreType.DMA
    anywhere = pl.BlockSpec(memory_space=pl.ANY)
    local = pl.BlockSpec(memory_space=pltpu.VMEM)
    return pl.pallas_call(
        functools.partial(fused_kernel, n, groups),
        out_shape=jax.ShapeDtypeStruct((samples, count, width), bf16),
        in_specs=[anywhere] + [local] * 6 + [anywhere] * 6,
        out_specs=local,
        scratch_shapes=[
            pltpu.VMEM((samples * frames, patches, width), bf16),
            pltpu.VMEM((samples * frames, patches, width), bf16),
            pltpu.VMEM((LAYERS, samples, frames * patches, 2 * inner), bf16),
            pltpu.VMEM((LAYERS, width, 3 * inner), bf16),
            pltpu.VMEM((LAYERS, inner, width), bf16),
            pltpu.VMEM((LAYERS, width, hidden), bf16),
            pltpu.VMEM((LAYERS, hidden, width), bf16),
            pltpu.VMEM((samples * count, width), jnp.float32),
            pltpu.VMEM((2 * LAYERS, groups, rows_each, width), bf16),
            pltpu.VMEM((2 * LAYERS, groups - 1, rows_each, width), bf16),
            pltpu.VMEM((2 * LAYERS, groups, rows_each, width), bf16),
            dma((samples * frames,)),
            dma((units, 3)),
            dma((units, ring, 2, 2)),
            dma((units, ring, 2)),
            dma((2 * LAYERS, groups - 1)),
            dma((2 * LAYERS, groups - 1)),
            dma((2 * LAYERS, groups - 1)),
            dma((2 * LAYERS, groups - 1)),
        ],
        compiler_params=pltpu.CompilerParams(
            collective_id=0, has_side_effects=True, vmem_limit_bytes=60 * 2**20
        ),
    )(media, latents, time_embed.astype(jnp.float32), media_gain, latent_gain, ffn_gain, out_gain[None],
      w_query, w_key, w_value, w_out, w_up, w_down)


def choose(n, groups, *args):
    if n >= 4 and n % 2 == 0 and args[7].shape[1] % 128 == 0 and args[7].shape[2] == 128:
        return fused(n, groups, *args)
    return on_device(*args)


def solution(mesh):
    in_specs = (
        P("dp", None, None, None),
        P(),
        P(),
        P(),
        P(),
        P(),
        P(),
        P(None, "dp", "mp"),
        P(None, "dp", "mp"),
        P(None, "dp", "mp"),
        P(None, "mp", "dp"),
        P(None, "dp", "mp"),
        P(None, "mp", "dp"),
    )
    out_specs = P("dp", None, None)
    body = functools.partial(choose, mesh.shape["dp"], mesh.shape["mp"])
    return jax.shard_map(
        body, mesh=mesh, in_specs=in_specs, out_specs=out_specs, check_vma=False
    )
```

```python
import functools

import jax
import jax.numpy as jnp
from jax import lax
from jax.experimental import pallas as pl
from jax.experimental.pallas import tpu as pltpu
from jax.sharding import PartitionSpec as P

MESH = pl.DeviceIdType.MESH

HEAD = 64
LAYERS = 2
LEAD = 1
PARTS = 4
AHEAD = 2


def layer_norm(values, gain):
    center = values - jnp.mean(values, axis=-1, keepdims=True)
    spread = jnp.mean(center * center, axis=-1, keepdims=True)
    return center * lax.rsqrt(spread + 1e-05) * gain


def matmul(left, right):
    return jnp.dot(left, right, preferred_element_type=jnp.float32)


def on_device(
    media,
    latents,
    time_embed,
    media_gain,
    latent_gain,
    ffn_gain,
    out_gain,
    w_query,
    w_key,
    w_value,
    w_out,
    w_up,
    w_down,
):
    samples = media.shape[0]
    frames = media.shape[1]
    patches = media.shape[2]
    width = media.shape[3]
    count = latents.shape[0]
    head_size = HEAD
    local_heads = w_query.shape[2] // head_size
    scale = head_size ** (-0.5)
    tokens = frames * patches
    flat = (media.astype(jnp.float32) + time_embed.astype(jnp.float32)[None, :, None, :]).reshape(
        samples * tokens, width
    )
    state = jnp.broadcast_to(latents.astype(jnp.float32)[None], (samples, count, width)).reshape(
        samples * count, width
    )
    row_parts = (
        lax.all_gather(w_query, "dp", axis=1, tiled=True),
        lax.all_gather(w_key, "dp", axis=1, tiled=True),
        lax.all_gather(w_value, "dp", axis=1, tiled=True),
        lax.all_gather(w_up, "dp", axis=1, tiled=True),
    )
    col_parts = (
        lax.all_gather(w_out, "dp", axis=2, tiled=True),
        lax.all_gather(w_down, "dp", axis=2, tiled=True),
    )

    def full_rows(values, gain):
        normed = layer_norm(values, gain).astype(jnp.bfloat16)
        return normed

    def add_update(current, partial_value):
        return current + lax.psum(partial_value.astype(jnp.bfloat16), "mp").astype(jnp.float32)

    for layer in range(LAYERS):
        query_weight = row_parts[0][layer]
        key_weight = row_parts[1][layer]
        value_weight = row_parts[2][layer]
        up_weight = row_parts[3][layer]
        out_weight = col_parts[0][layer]
        down_weight = col_parts[1][layer]
        media_normed = layer_norm(flat, media_gain[layer]).astype(jnp.bfloat16)
        latent_normed = full_rows(state, latent_gain[layer])
        query = matmul(latent_normed, query_weight)
        key_media = matmul(media_normed, key_weight)
        value_media = matmul(media_normed, value_weight)
        key_latent = matmul(latent_normed, key_weight)
        value_latent = matmul(latent_normed, value_weight)
        queries = (
            (query * scale).astype(jnp.bfloat16).reshape(samples, count, local_heads, head_size)
        )
        keys = jnp.concatenate(
            [
                key_media.astype(jnp.bfloat16).reshape(samples, tokens, local_heads, head_size),
                key_latent.astype(jnp.bfloat16).reshape(samples, count, local_heads, head_size),
            ],
            axis=1,
        )
        values = jnp.concatenate(
            [
                value_media.astype(jnp.bfloat16).reshape(samples, tokens, local_heads, head_size),
                value_latent.astype(jnp.bfloat16).reshape(samples, count, local_heads, head_size),
            ],
            axis=1,
        )
        scores = jnp.einsum("sqhd,skhd->shqk", queries, keys, preferred_element_type=jnp.float32)
        probs = jax.nn.softmax(scores, axis=-1).astype(jnp.bfloat16)
        attended = jnp.einsum("shqk,skhd->sqhd", probs, values, preferred_element_type=jnp.float32)
        attended = attended.astype(jnp.bfloat16).reshape(samples * count, local_heads * head_size)
        state = add_update(state, matmul(attended, out_weight))
        ffn_normed = full_rows(state, ffn_gain[layer])
        hidden = jax.nn.gelu(matmul(ffn_normed, up_weight), approximate=False).astype(jnp.bfloat16)
        state = add_update(state, matmul(hidden, down_weight))
    final = layer_norm(state, out_gain).astype(jnp.bfloat16)
    return final.reshape(samples, count, width)


def fused_kernel(
    n, groups,
    media, latents, time_embed, media_gain, latent_gain, ffn_gain, out_gain,
    w_query, w_key, w_value, w_out, w_up, w_down,
    out,
    frames_in, normed_next, kv, g_qkv, g_out, g_up, g_down, state,
    part, rs_in, ag_in,
    media_sem, own_sem, send_sem, recv_sem, rs_send, rs_recv, ag_send, ag_recv,
):
    samples, frames, patches, width = media.shape
    count = latents.shape[0]
    tokens = frames * patches
    inner = w_query.shape[2]
    heads = inner // HEAD
    depth = w_query.shape[1]
    hidden = w_up.shape[2]
    half = hidden // 2
    ring = n // 2
    me = lax.axis_index("dp")
    mine = lax.axis_index("mp")
    along, across = me // 2, me % 2

    def index(a, b):
        return lax.rem(a + 2 * ring, ring) * 2 + b

    for target in (index(along, 1 - across), index(along + 1, across), index(along - 1, across)):
        pl.semaphore_signal(pltpu.get_barrier_semaphore(), inc=1, device_id={"dp": target}, device_id_type=MESH)
    for k in range(1, groups):
        pl.semaphore_signal(
            pltpu.get_barrier_semaphore(), inc=1, device_id={"mp": lax.rem(mine + k, groups)}, device_id_type=MESH
        )

    units = []
    for layer in range(LAYERS):
        if layer == 0:
            units += [("qkv", 0, 0), ("qkv", 1, 1)]
        units += [("out", layer, layer), ("up", layer, 0), ("up", layer, 1), ("down", layer, 0), ("down", layer, 1)]
    where = {unit: i for i, unit in enumerate(units)}

    def span(origin, size):
        return pl.ds(pl.multiple_of(origin * size, size), size)

    def piece(u, origin):
        kind, layer, part_of = units[u]
        if kind == "qkv":
            return g_qkv.at[layer, span(origin, depth), :]
        if kind == "out":
            return g_out.at[layer, :, span(origin, depth)]
        if kind == "up":
            return g_up.at[layer, span(origin, depth), pl.ds(part_of * half, half)]
        return g_down.at[layer, pl.ds(part_of * half, half), span(origin, depth)]

    def own_copies(u):
        kind, layer, part_of = units[u]
        if kind == "qkv":
            return [
                pltpu.make_async_copy(
                    w.at[layer], g_qkv.at[layer, span(me, depth), pl.ds(i * inner, inner)], own_sem.at[u, i]
                )
                for i, w in enumerate((w_query, w_key, w_value))
            ]
        if kind == "out":
            source = w_out.at[layer]
        elif kind == "up":
            source = w_up.at[layer, :, pl.ds(part_of * half, half)]
        else:
            source = w_down.at[layer, pl.ds(part_of * half, half), :]
        return [pltpu.make_async_copy(source, piece(u, me), own_sem.at[u, 0])]

    def turn(u):
        return 1 if units[u][2] == 0 else -1

    def sending(u, s, other, to_ring):
        r = turn(u)
        ref = piece(u, index(along - r * s, 1 - across if other else across))
        if to_ring:
            target, slot = index(along + r, across), recv_sem.at[u, s + 1, other]
        else:
            target, slot = index(along, 1 - across), recv_sem.at[u, s, 1 - other]
        return pltpu.make_async_remote_copy(
            src_ref=ref, dst_ref=ref, send_sem=send_sem.at[u, s, other, int(to_ring)], recv_sem=slot,
            device_id={"dp": target}, device_id_type=MESH,
        )

    started = []

    def send(*which):
        copy = sending(*which)
        copy.start()
        started.append(copy)

    def arrived(u, s, other):
        r = turn(u)
        ref = piece(u, index(along - r * s, 1 - across if other else across))
        pltpu.make_async_remote_copy(
            src_ref=ref, dst_ref=ref, send_sem=send_sem.at[u, s, other, 0], recv_sem=recv_sem.at[u, s, other],
            device_id={"dp": index(along, 1 - across)}, device_id_type=MESH,
        ).wait_recv()

    def pair_first(u):
        return units[u][0] == "up" and units[u][2] == 1

    def event(u, s):
        if s == 0:
            for copy in own_copies(u):
                copy.wait()
            send(u, 0, 0, True)
            send(u, 0, 0, False)
            return
        if pair_first(u):
            arrived(u, s - 1, 1)
            send(u, s - 1, 1, True)
            arrived(u, s, 0)
            if s < ring - 1:
                send(u, s, 0, True)
        else:
            arrived(u, s, 0)
            if s < ring - 1:
                send(u, s, 0, True)
            send(u, s, 0, False)

    def complete(u):
        if pair_first(u):
            arrived(u, ring - 1, 1)
        else:
            for s in range(ring):
                arrived(u, s, 1)

    slots = {}
    for u in range(len(units)):
        for s in range(ring):
            slots.setdefault(u + s + 0 if s else max(0, u - LEAD), []).append((u, s))
    clock = [0]

    def advance(until):
        while clock[0] <= until:
            for u, s in sorted(slots.get(clock[0], []), key=lambda e: (e[1] > 0, e[0])):
                event(u, s)
            clock[0] += 1

    def need(*unit):
        u = where[unit]
        advance(u + ring - 1 + 0 + AHEAD)
        complete(u)

    for u in range(len(units)):
        for copy in own_copies(u):
            copy.start()

    def frame_copy(i):
        return pltpu.make_async_copy(media.at[i // frames, i % frames], frames_in.at[i], media_sem.at[i])

    @pl.loop(0, samples * frames)
    def _(i):
        frame_copy(i).start()

    pl.semaphore_wait(pltpu.get_barrier_semaphore(), 3 + groups - 1)
    advance(0)

    state[...] = jnp.concatenate([latents[...].astype(jnp.float32)] * samples, axis=0)

    def norm_frames(low, high):
        @pl.loop(low, high)
        def _(i):
            frame_copy(i).wait()

            @pl.loop(0, patches // 64)
            def _(j):
                rows = pl.ds(pl.multiple_of(j * 64, 64), 64)
                flat = frames_in[i, rows, :].astype(jnp.float32) + time_embed[pl.ds(lax.rem(i, frames), 1), :]
                center = flat - jnp.mean(flat, axis=-1, keepdims=True)
                spread = jnp.mean(center * center, axis=-1, keepdims=True)
                scaled = center * lax.rsqrt(spread + 1e-05)
                frames_in[i, rows, :] = (scaled * media_gain[0:1, :]).astype(jnp.bfloat16)
                normed_next[i, rows, :] = (scaled * media_gain[1:2, :]).astype(jnp.bfloat16)

    def project(layer):
        normed = frames_in if layer == 0 else normed_next

        @pl.loop(0, samples * frames)
        def _(i):
            both = matmul(normed[i], g_qkv[layer, :, inner : 3 * inner])
            rows = pl.ds(pl.multiple_of(lax.rem(i, frames) * patches, patches), patches)
            kv[layer, i // frames, rows, :] = both.astype(jnp.bfloat16)

    def attend(layer):
        normed = layer_norm(state[...], latent_gain[layer : layer + 1, :]).astype(jnp.bfloat16)
        own = matmul(normed, g_qkv[layer])
        queries = (own[:, :inner] * (HEAD ** (-0.5))).astype(jnp.bfloat16)
        own_kv = own[:, inner:].astype(jnp.bfloat16)
        lane = lax.broadcasted_iota(jnp.int32, (count, inner), 1) // HEAD
        dims = (((1,), (1,)), ((), ()))
        results = []
        for b in range(samples):
            q = queries[b * count : (b + 1) * count]
            stacked = jnp.concatenate([jnp.where(lane == h, q, jnp.zeros_like(q)) for h in range(heads)], axis=0)
            k_own = own_kv[b * count : (b + 1) * count, :inner]
            v_own = own_kv[b * count : (b + 1) * count, inner:]
            s_far = lax.dot_general(stacked, kv[layer, b, :, :inner], dims, preferred_element_type=jnp.float32)
            s_own = lax.dot_general(stacked, k_own, dims, preferred_element_type=jnp.float32)
            top = jnp.maximum(jnp.max(s_far, axis=-1, keepdims=True), jnp.max(s_own, axis=-1, keepdims=True))
            e_far, e_own = jnp.exp(s_far - top), jnp.exp(s_own - top)
            total = jnp.sum(e_far, axis=-1, keepdims=True) + jnp.sum(e_own, axis=-1, keepdims=True)
            inverse = 1.0 / total
            mixed = matmul((e_far * inverse).astype(jnp.bfloat16), kv[layer, b, :, inner:])
            mixed += matmul((e_own * inverse).astype(jnp.bfloat16), v_own)
            result = mixed[:count]
            for h in range(1, heads):
                result = jnp.where(lane == h, mixed[h * count : (h + 1) * count], result)
            results.append(result.astype(jnp.bfloat16))
        return jnp.concatenate(results, axis=0)

    rows_each = samples * count // groups

    def add_update(a, update):
        part[a] = update.astype(jnp.bfloat16).reshape(groups, rows_each, width)
        first = []
        for k in range(1, groups):
            peer = lax.rem(mine + k, groups)
            copy = pltpu.make_async_remote_copy(
                src_ref=part.at[a, peer], dst_ref=rs_in.at[a, k - 1],
                send_sem=rs_send.at[a, k - 1], recv_sem=rs_recv.at[a, k - 1],
                device_id={"mp": peer}, device_id_type=MESH,
            )
            copy.start()
            started.append(copy)
            first.append(copy)
        advance(clock[0])
        total = part[a, mine].astype(jnp.float32)
        for k, copy in enumerate(first):
            copy.wait_recv()
            total += rs_in[a, k].astype(jnp.float32)
        ag_in[a, mine] = total.astype(jnp.bfloat16)
        second = []
        for k in range(1, groups):
            copy = pltpu.make_async_remote_copy(
                src_ref=ag_in.at[a, mine], dst_ref=ag_in.at[a, mine],
                send_sem=ag_send.at[a, k - 1], recv_sem=ag_recv.at[a, k - 1],
                device_id={"mp": lax.rem(mine + k, groups)}, device_id_type=MESH,
            )
            copy.start()
            started.append(copy)
            second.append(copy)
        advance(clock[0])
        for copy in second:
            copy.wait_recv()
        state[...] += ag_in[a].astype(jnp.float32).reshape(samples * count, width)

    block = samples * frames // PARTS
    for i in range(PARTS):
        norm_frames(i * block, (i + 1) * block)
        advance(i + 1)
    for layer in range(LAYERS):
        if layer == 0:
            need("qkv", 0, 0)
            project(0)
        attended = attend(layer)
        if layer == 0:
            need("qkv", 1, 1)
            project(1)
        need("out", layer, layer)
        add_update(2 * layer, matmul(attended, g_out[layer]))
        normed = layer_norm(state[...], ffn_gain[layer : layer + 1, :]).astype(jnp.bfloat16)
        active = []
        for h in range(2):
            need("up", layer, h)
            value = matmul(normed, g_up[layer, :, h * half : (h + 1) * half])
            active.append((0.5 * value * (1.0 + lax.erf(value * (0.5**0.5)))).astype(jnp.bfloat16))
        update = None
        for h in range(2):
            need("down", layer, h)
            term = matmul(active[h], g_down[layer, h * half : (h + 1) * half, :])
            update = term if update is None else update + term
        add_update(2 * layer + 1, update)
    final = layer_norm(state[...], out_gain[...]).astype(jnp.bfloat16)
    out[...] = final.reshape(samples, count, width)
    for copy in started:
        copy.wait_send()


def fused(n, groups, media, latents, time_embed, media_gain, latent_gain, ffn_gain, out_gain,
          w_query, w_key, w_value, w_out, w_up, w_down):
    samples, frames, patches, width = media.shape
    count = latents.shape[0]
    inner = w_query.shape[2]
    hidden = w_up.shape[2]
    ring = n // 2
    rows_each = samples * count // groups
    units = LAYERS * 6
    bf16 = jnp.bfloat16
    dma = pltpu.SemaphoreType.DMA
    anywhere = pl.BlockSpec(memory_space=pl.ANY)
    local = pl.BlockSpec(memory_space=pltpu.VMEM)
    return pl.pallas_call(
        functools.partial(fused_kernel, n, groups),
        out_shape=jax.ShapeDtypeStruct((samples, count, width), bf16),
        in_specs=[anywhere] + [local] * 6 + [anywhere] * 6,
        out_specs=local,
        scratch_shapes=[
            pltpu.VMEM((samples * frames, patches, width), bf16),
            pltpu.VMEM((samples * frames, patches, width), bf16),
            pltpu.VMEM((LAYERS, samples, frames * patches, 2 * inner), bf16),
            pltpu.VMEM((LAYERS, width, 3 * inner), bf16),
            pltpu.VMEM((LAYERS, inner, width), bf16),
            pltpu.VMEM((LAYERS, width, hidden), bf16),
            pltpu.VMEM((LAYERS, hidden, width), bf16),
            pltpu.VMEM((samples * count, width), jnp.float32),
            pltpu.VMEM((2 * LAYERS, groups, rows_each, width), bf16),
            pltpu.VMEM((2 * LAYERS, groups - 1, rows_each, width), bf16),
            pltpu.VMEM((2 * LAYERS, groups, rows_each, width), bf16),
            dma((samples * frames,)),
            dma((units, 3)),
            dma((units, ring, 2, 2)),
            dma((units, ring, 2)),
            dma((2 * LAYERS, groups - 1)),
            dma((2 * LAYERS, groups - 1)),
            dma((2 * LAYERS, groups - 1)),
            dma((2 * LAYERS, groups - 1)),
        ],
        compiler_params=pltpu.CompilerParams(
            collective_id=0, has_side_effects=True, vmem_limit_bytes=60 * 2**20
        ),
    )(media, latents, time_embed.astype(jnp.float32), media_gain, latent_gain, ffn_gain, out_gain[None],
      w_query, w_key, w_value, w_out, w_up, w_down)


def choose(n, groups, *args):
    if n >= 4 and n % 2 == 0 and args[7].shape[1] % 128 == 0 and args[7].shape[2] == 128:
        return fused(n, groups, *args)
    return on_device(*args)


def solution(mesh):
    in_specs = (
        P("dp", None, None, None),
        P(),
        P(),
        P(),
        P(),
        P(),
        P(),
        P(None, "dp", "mp"),
        P(None, "dp", "mp"),
        P(None, "dp", "mp"),
        P(None, "mp", "dp"),
        P(None, "dp", "mp"),
        P(None, "mp", "dp"),
    )
    out_specs = P("dp", None, None)
    body = functools.partial(choose, mesh.shape["dp"], mesh.shape["mp"])
    return jax.shard_map(
        body, mesh=mesh, in_specs=in_specs, out_specs=out_specs, check_vma=False
    )
```

```python
import functools

import jax
import jax.numpy as jnp
from jax import lax
from jax.experimental import pallas as pl
from jax.experimental.pallas import tpu as pltpu
from jax.sharding import PartitionSpec as P

MESH = pl.DeviceIdType.MESH

HEAD = 64
LAYERS = 2
LEAD = 1
PARTS = 4
AHEAD = 2


def layer_norm(values, gain):
    center = values - jnp.mean(values, axis=-1, keepdims=True)
    spread = jnp.mean(center * center, axis=-1, keepdims=True)
    return center * lax.rsqrt(spread + 1e-05) * gain


def matmul(left, right):
    return jnp.dot(left, right, preferred_element_type=jnp.float32)


def on_device(
    media,
    latents,
    time_embed,
    media_gain,
    latent_gain,
    ffn_gain,
    out_gain,
    w_query,
    w_key,
    w_value,
    w_out,
    w_up,
    w_down,
):
    samples = media.shape[0]
    frames = media.shape[1]
    patches = media.shape[2]
    width = media.shape[3]
    count = latents.shape[0]
    head_size = HEAD
    local_heads = w_query.shape[2] // head_size
    scale = head_size ** (-0.5)
    tokens = frames * patches
    flat = (media.astype(jnp.float32) + time_embed.astype(jnp.float32)[None, :, None, :]).reshape(
        samples * tokens, width
    )
    state = jnp.broadcast_to(latents.astype(jnp.float32)[None], (samples, count, width)).reshape(
        samples * count, width
    )
    row_parts = (
        lax.all_gather(w_query, "dp", axis=1, tiled=True),
        lax.all_gather(w_key, "dp", axis=1, tiled=True),
        lax.all_gather(w_value, "dp", axis=1, tiled=True),
        lax.all_gather(w_up, "dp", axis=1, tiled=True),
    )
    col_parts = (
        lax.all_gather(w_out, "dp", axis=2, tiled=True),
        lax.all_gather(w_down, "dp", axis=2, tiled=True),
    )

    def full_rows(values, gain):
        normed = layer_norm(values, gain).astype(jnp.bfloat16)
        return normed

    def add_update(current, partial_value):
        return current + lax.psum(partial_value.astype(jnp.bfloat16), "mp").astype(jnp.float32)

    for layer in range(LAYERS):
        query_weight = row_parts[0][layer]
        key_weight = row_parts[1][layer]
        value_weight = row_parts[2][layer]
        up_weight = row_parts[3][layer]
        out_weight = col_parts[0][layer]
        down_weight = col_parts[1][layer]
        media_normed = layer_norm(flat, media_gain[layer]).astype(jnp.bfloat16)
        latent_normed = full_rows(state, latent_gain[layer])
        query = matmul(latent_normed, query_weight)
        key_media = matmul(media_normed, key_weight)
        value_media = matmul(media_normed, value_weight)
        key_latent = matmul(latent_normed, key_weight)
        value_latent = matmul(latent_normed, value_weight)
        queries = (
            (query * scale).astype(jnp.bfloat16).reshape(samples, count, local_heads, head_size)
        )
        keys = jnp.concatenate(
            [
                key_media.astype(jnp.bfloat16).reshape(samples, tokens, local_heads, head_size),
                key_latent.astype(jnp.bfloat16).reshape(samples, count, local_heads, head_size),
            ],
            axis=1,
        )
        values = jnp.concatenate(
            [
                value_media.astype(jnp.bfloat16).reshape(samples, tokens, local_heads, head_size),
                value_latent.astype(jnp.bfloat16).reshape(samples, count, local_heads, head_size),
            ],
            axis=1,
        )
        scores = jnp.einsum("sqhd,skhd->shqk", queries, keys, preferred_element_type=jnp.float32)
        probs = jax.nn.softmax(scores, axis=-1).astype(jnp.bfloat16)
        attended = jnp.einsum("shqk,skhd->sqhd", probs, values, preferred_element_type=jnp.float32)
        attended = attended.astype(jnp.bfloat16).reshape(samples * count, local_heads * head_size)
        state = add_update(state, matmul(attended, out_weight))
        ffn_normed = full_rows(state, ffn_gain[layer])
        hidden = jax.nn.gelu(matmul(ffn_normed, up_weight), approximate=False).astype(jnp.bfloat16)
        state = add_update(state, matmul(hidden, down_weight))
    final = layer_norm(state, out_gain).astype(jnp.bfloat16)
    return final.reshape(samples, count, width)


def fused_kernel(
    n, groups,
    media, latents, time_embed, media_gain, latent_gain, ffn_gain, out_gain,
    w_query, w_key, w_value, w_out, w_up, w_down,
    out,
    frames_in, normed_next, kv, g_qkv, g_out, g_up, g_down, state,
    part, rs_in, ag_in,
    media_sem, own_sem, send_sem, recv_sem, rs_send, rs_recv, ag_send, ag_recv,
):
    samples, frames, patches, width = media.shape
    count = latents.shape[0]
    tokens = frames * patches
    inner = w_query.shape[2]
    heads = inner // HEAD
    depth = w_query.shape[1]
    hidden = w_up.shape[2]
    half = hidden // 2
    ring = n // 2
    me = lax.axis_index("dp")
    mine = lax.axis_index("mp")
    along, across = me // 2, me % 2

    def index(a, b):
        return lax.rem(a + 2 * ring, ring) * 2 + b

    for target in (index(along, 1 - across), index(along + 1, across), index(along - 1, across)):
        pl.semaphore_signal(pltpu.get_barrier_semaphore(), inc=1, device_id={"dp": target}, device_id_type=MESH)
    for k in range(1, groups):
        pl.semaphore_signal(
            pltpu.get_barrier_semaphore(), inc=1, device_id={"mp": lax.rem(mine + k, groups)}, device_id_type=MESH
        )

    units = []
    for layer in range(LAYERS):
        if layer == 0:
            units += [("qkv", 0, 0), ("qkv", 1, 1)]
        units += [("out", layer, layer), ("up", layer, 0), ("up", layer, 1), ("down", layer, 0), ("down", layer, 1)]
    where = {unit: i for i, unit in enumerate(units)}

    def span(origin, size):
        return pl.ds(pl.multiple_of(origin * size, size), size)

    def piece(u, origin):
        kind, layer, part_of = units[u]
        if kind == "qkv":
            return g_qkv.at[layer, span(origin, depth), :]
        if kind == "out":
            return g_out.at[layer, :, span(origin, depth)]
        if kind == "up":
            return g_up.at[layer, span(origin, depth), pl.ds(part_of * half, half)]
        return g_down.at[layer, pl.ds(part_of * half, half), span(origin, depth)]

    def own_copies(u):
        kind, layer, part_of = units[u]
        if kind == "qkv":
            return [
                pltpu.make_async_copy(
                    w.at[layer], g_qkv.at[layer, span(me, depth), pl.ds(i * inner, inner)], own_sem.at[u, i]
                )
                for i, w in enumerate((w_query, w_key, w_value))
            ]
        if kind == "out":
            source = w_out.at[layer]
        elif kind == "up":
            source = w_up.at[layer, :, pl.ds(part_of * half, half)]
        else:
            source = w_down.at[layer, pl.ds(part_of * half, half), :]
        return [pltpu.make_async_copy(source, piece(u, me), own_sem.at[u, 0])]

    def turn(u):
        return 1

    def sending(u, s, other, to_ring):
        r = turn(u)
        ref = piece(u, index(along - r * s, 1 - across if other else across))
        if to_ring:
            target, slot = index(along + r, across), recv_sem.at[u, s + 1, other]
        else:
            target, slot = index(along, 1 - across), recv_sem.at[u, s, 1 - other]
        return pltpu.make_async_remote_copy(
            src_ref=ref, dst_ref=ref, send_sem=send_sem.at[u, s, other, int(to_ring)], recv_sem=slot,
            device_id={"dp": target}, device_id_type=MESH,
        )

    started = []

    def send(*which):
        copy = sending(*which)
        copy.start()
        started.append(copy)

    def arrived(u, s, other):
        r = turn(u)
        ref = piece(u, index(along - r * s, 1 - across if other else across))
        pltpu.make_async_remote_copy(
            src_ref=ref, dst_ref=ref, send_sem=send_sem.at[u, s, other, 0], recv_sem=recv_sem.at[u, s, other],
            device_id={"dp": index(along, 1 - across)}, device_id_type=MESH,
        ).wait_recv()

    def pair_first(u):
        return units[u][0] == "up" and units[u][2] == 1

    def event(u, s):
        if s == 0:
            for copy in own_copies(u):
                copy.wait()
            send(u, 0, 0, True)
            send(u, 0, 0, False)
            return
        if pair_first(u):
            arrived(u, s - 1, 1)
            send(u, s - 1, 1, True)
            arrived(u, s, 0)
            if s < ring - 1:
                send(u, s, 0, True)
        else:
            arrived(u, s, 0)
            if s < ring - 1:
                send(u, s, 0, True)
            send(u, s, 0, False)

    def complete(u):
        if pair_first(u):
            arrived(u, ring - 1, 1)
        else:
            for s in range(ring):
                arrived(u, s, 1)

    slots = {}
    for u in range(len(units)):
        for s in range(ring):
            slots.setdefault(u + s + 0 if s else max(0, u - LEAD), []).append((u, s))
    clock = [0]

    def advance(until):
        while clock[0] <= until:
            for u, s in sorted(slots.get(clock[0], []), key=lambda e: (e[1] > 0, e[0])):
                event(u, s)
            clock[0] += 1

    def need(*unit):
        u = where[unit]
        advance(u + ring - 1 + 0 + AHEAD)
        complete(u)

    for u in range(len(units)):
        for copy in own_copies(u):
            copy.start()

    def frame_copy(i):
        return pltpu.make_async_copy(media.at[i // frames, i % frames], frames_in.at[i], media_sem.at[i])

    @pl.loop(0, samples * frames)
    def _(i):
        frame_copy(i).start()

    pl.semaphore_wait(pltpu.get_barrier_semaphore(), 3 + groups - 1)
    advance(0)

    state[...] = jnp.concatenate([latents[...].astype(jnp.float32)] * samples, axis=0)

    def norm_frames(low, high):
        @pl.loop(low, high)
        def _(i):
            frame_copy(i).wait()

            @pl.loop(0, patches // 64)
            def _(j):
                rows = pl.ds(pl.multiple_of(j * 64, 64), 64)
                flat = frames_in[i, rows, :].astype(jnp.float32) + time_embed[pl.ds(lax.rem(i, frames), 1), :]
                center = flat - jnp.mean(flat, axis=-1, keepdims=True)
                spread = jnp.mean(center * center, axis=-1, keepdims=True)
                scaled = center * lax.rsqrt(spread + 1e-05)
                frames_in[i, rows, :] = (scaled * media_gain[0:1, :]).astype(jnp.bfloat16)
                normed_next[i, rows, :] = (scaled * media_gain[1:2, :]).astype(jnp.bfloat16)

    def project(layer):
        normed = frames_in if layer == 0 else normed_next

        @pl.loop(0, samples * frames)
        def _(i):
            both = matmul(normed[i], g_qkv[layer, :, inner : 3 * inner])
            rows = pl.ds(pl.multiple_of(lax.rem(i, frames) * patches, patches), patches)
            kv[layer, i // frames, rows, :] = both.astype(jnp.bfloat16)

    def attend(layer):
        normed = layer_norm(state[...], latent_gain[layer : layer + 1, :]).astype(jnp.bfloat16)
        own = matmul(normed, g_qkv[layer])
        queries = (own[:, :inner] * (HEAD ** (-0.5))).astype(jnp.bfloat16)
        own_kv = own[:, inner:].astype(jnp.bfloat16)
        lane = lax.broadcasted_iota(jnp.int32, (count, inner), 1) // HEAD
        dims = (((1,), (1,)), ((), ()))
        results = []
        for b in range(samples):
            q = queries[b * count : (b + 1) * count]
            stacked = jnp.concatenate([jnp.where(lane == h, q, jnp.zeros_like(q)) for h in range(heads)], axis=0)
            k_own = own_kv[b * count : (b + 1) * count, :inner]
            v_own = own_kv[b * count : (b + 1) * count, inner:]
            s_far = lax.dot_general(stacked, kv[layer, b, :, :inner], dims, preferred_element_type=jnp.float32)
            s_own = lax.dot_general(stacked, k_own, dims, preferred_element_type=jnp.float32)
            top = jnp.maximum(jnp.max(s_far, axis=-1, keepdims=True), jnp.max(s_own, axis=-1, keepdims=True))
            e_far, e_own = jnp.exp(s_far - top), jnp.exp(s_own - top)
            total = jnp.sum(e_far, axis=-1, keepdims=True) + jnp.sum(e_own, axis=-1, keepdims=True)
            inverse = 1.0 / total
            mixed = matmul((e_far * inverse).astype(jnp.bfloat16), kv[layer, b, :, inner:])
            mixed += matmul((e_own * inverse).astype(jnp.bfloat16), v_own)
            result = mixed[:count]
            for h in range(1, heads):
                result = jnp.where(lane == h, mixed[h * count : (h + 1) * count], result)
            results.append(result.astype(jnp.bfloat16))
        return jnp.concatenate(results, axis=0)

    rows_each = samples * count // groups

    def add_update(a, update):
        part[a] = update.astype(jnp.bfloat16).reshape(groups, rows_each, width)
        first = []
        for k in range(1, groups):
            peer = lax.rem(mine + k, groups)
            copy = pltpu.make_async_remote_copy(
                src_ref=part.at[a, peer], dst_ref=rs_in.at[a, k - 1],
                send_sem=rs_send.at[a, k - 1], recv_sem=rs_recv.at[a, k - 1],
                device_id={"mp": peer}, device_id_type=MESH,
            )
            copy.start()
            started.append(copy)
            first.append(copy)
        advance(clock[0])
        total = part[a, mine].astype(jnp.float32)
        for k, copy in enumerate(first):
            copy.wait_recv()
            total += rs_in[a, k].astype(jnp.float32)
        ag_in[a, mine] = total.astype(jnp.bfloat16)
        second = []
        for k in range(1, groups):
            copy = pltpu.make_async_remote_copy(
                src_ref=ag_in.at[a, mine], dst_ref=ag_in.at[a, mine],
                send_sem=ag_send.at[a, k - 1], recv_sem=ag_recv.at[a, k - 1],
                device_id={"mp": lax.rem(mine + k, groups)}, device_id_type=MESH,
            )
            copy.start()
            started.append(copy)
            second.append(copy)
        advance(clock[0])
        for copy in second:
            copy.wait_recv()
        state[...] += ag_in[a].astype(jnp.float32).reshape(samples * count, width)

    block = samples * frames // PARTS
    for i in range(PARTS):
        norm_frames(i * block, (i + 1) * block)
        advance(i + 1)
    for layer in range(LAYERS):
        if layer == 0:
            need("qkv", 0, 0)
            project(0)
        attended = attend(layer)
        if layer == 0:
            need("qkv", 1, 1)
            project(1)
        need("out", layer, layer)
        add_update(2 * layer, matmul(attended, g_out[layer]))
        normed = layer_norm(state[...], ffn_gain[layer : layer + 1, :]).astype(jnp.bfloat16)
        active = []
        for h in range(2):
            need("up", layer, h)
            value = matmul(normed, g_up[layer, :, h * half : (h + 1) * half])
            active.append((0.5 * value * (1.0 + lax.erf(value * (0.5**0.5)))).astype(jnp.bfloat16))
        update = None
        for h in range(2):
            need("down", layer, h)
            term = matmul(active[h], g_down[layer, h * half : (h + 1) * half, :])
            update = term if update is None else update + term
        add_update(2 * layer + 1, update)
    final = layer_norm(state[...], out_gain[...]).astype(jnp.bfloat16)
    out[...] = final.reshape(samples, count, width)
    for copy in started:
        copy.wait_send()


def fused(n, groups, media, latents, time_embed, media_gain, latent_gain, ffn_gain, out_gain,
          w_query, w_key, w_value, w_out, w_up, w_down):
    samples, frames, patches, width = media.shape
    count = latents.shape[0]
    inner = w_query.shape[2]
    hidden = w_up.shape[2]
    ring = n // 2
    rows_each = samples * count // groups
    units = LAYERS * 6
    bf16 = jnp.bfloat16
    dma = pltpu.SemaphoreType.DMA
    anywhere = pl.BlockSpec(memory_space=pl.ANY)
    local = pl.BlockSpec(memory_space=pltpu.VMEM)
    return pl.pallas_call(
        functools.partial(fused_kernel, n, groups),
        out_shape=jax.ShapeDtypeStruct((samples, count, width), bf16),
        in_specs=[anywhere] + [local] * 6 + [anywhere] * 6,
        out_specs=local,
        scratch_shapes=[
            pltpu.VMEM((samples * frames, patches, width), bf16),
            pltpu.VMEM((samples * frames, patches, width), bf16),
            pltpu.VMEM((LAYERS, samples, frames * patches, 2 * inner), bf16),
            pltpu.VMEM((LAYERS, width, 3 * inner), bf16),
            pltpu.VMEM((LAYERS, inner, width), bf16),
            pltpu.VMEM((LAYERS, width, hidden), bf16),
            pltpu.VMEM((LAYERS, hidden, width), bf16),
            pltpu.VMEM((samples * count, width), jnp.float32),
            pltpu.VMEM((2 * LAYERS, groups, rows_each, width), bf16),
            pltpu.VMEM((2 * LAYERS, groups - 1, rows_each, width), bf16),
            pltpu.VMEM((2 * LAYERS, groups, rows_each, width), bf16),
            dma((samples * frames,)),
            dma((units, 3)),
            dma((units, ring, 2, 2)),
            dma((units, ring, 2)),
            dma((2 * LAYERS, groups - 1)),
            dma((2 * LAYERS, groups - 1)),
            dma((2 * LAYERS, groups - 1)),
            dma((2 * LAYERS, groups - 1)),
        ],
        compiler_params=pltpu.CompilerParams(
            collective_id=0, has_side_effects=True, vmem_limit_bytes=60 * 2**20
        ),
    )(media, latents, time_embed.astype(jnp.float32), media_gain, latent_gain, ffn_gain, out_gain[None],
      w_query, w_key, w_value, w_out, w_up, w_down)


def choose(n, groups, *args):
    if n >= 4 and n % 2 == 0 and args[7].shape[1] % 128 == 0 and args[7].shape[2] == 128:
        return fused(n, groups, *args)
    return on_device(*args)


def solution(mesh):
    in_specs = (
        P("dp", None, None, None),
        P(),
        P(),
        P(),
        P(),
        P(),
        P(),
        P(None, "dp", "mp"),
        P(None, "dp", "mp"),
        P(None, "dp", "mp"),
        P(None, "mp", "dp"),
        P(None, "dp", "mp"),
        P(None, "mp", "dp"),
    )
    out_specs = P("dp", None, None)
    body = functools.partial(choose, mesh.shape["dp"], mesh.shape["mp"])
    return jax.shard_map(
        body, mesh=mesh, in_specs=in_specs, out_specs=out_specs, check_vma=False
    )
```
